32 devices in a mesh: dp: 2 (over y), row: 4 (over z), col: 4 (over x, core).
Axes of the slice: x: 2, y: 2, z: 4, core: 2. Of those that a mesh axis runs over, the one named last changes fastest.
Arguments:
- tokens: bfloat16 [128, 12288], P(('dp', 'row')), may hold values from -6 to 6
- cotangent: bfloat16 [128, 49152], P('dp', ('row', 'col')), may hold values from -6 to 6
- weight_blocks: bfloat16 [16, 96, 128, 128], P(('row', 'col')), may hold values from -0.125 to 0.125
- block_rows: int32 [16, 96], P(('row', 'col')), may hold values from 0 to 95, as said below
- block_cols: int32 [16, 96], P(('row', 'col')), may hold values from 0 to 23
- block_count: int32 [16], P(('row', 'col')), may hold values from 24 to 96, as said below
Outputs:
- hidden: bfloat16 [128, 49152], P('dp', ('row', 'col'))
- weight_grad: bfloat16 [16, 96, 128, 128], P(('row', 'col'), 'dp')
The draws below stay inside these ranges and needn't reach their ends.
Inputs may be any that keep to these rules, and one draw needn't show every extreme that they name: Within each shard, the pairs (block_rows, block_cols) of the live slots are distinct. `block_count`: some shard has all 96 slots live in every draw.
All inputs are finite; a program needn't handle non-finite values.
Results may differ from the reference program's by a relative error of at most 0.009.
Values may be sent and summed in bfloat16 or wider, within the bound.
No kernel may reach another device: no remote copies, remote signals or barrier semaphores. Data moves between devices by JAX's collectives and lax.ppermute only.
A program may use at most 64 MiB of HBM per device.

```python
import jax
import jax.numpy as jnp
from jax import lax

D = 12288
FF = 49152
BLK = 128
CAP = 96
SHARDS = 16
TOKENS = 128
N_DP = 2


def block_pairs(key):
    col_blocks = FF // (SHARDS * BLK)
    candidates = D // BLK * col_blocks
    keys = jax.random.split(jax.random.fold_in(key, 7), SHARDS)
    chosen = jax.vmap(lambda one_key: jax.random.permutation(one_key, candidates)[:CAP])(keys)
    chosen = chosen.astype(jnp.int32)
    return (chosen // col_blocks, chosen % col_blocks)


def draw_block_rows(key, part):
    return block_pairs(key)[0]


def draw_block_cols(key, part):
    return block_pairs(key)[1]


def draw_block_count(key, part):
    counts = jax.random.randint(jax.random.fold_in(key, 11), (SHARDS,), max(1, CAP // 4), CAP + 1).astype(jnp.int32)
    fullest = jax.random.randint(jax.random.fold_in(key, 13), (), 0, SHARDS)
    return counts.at[fullest].set(CAP)


def level_of(own_key, extent, cuts, least, top_value):
    gain, own = 1.0, jax.random.fold_in(own_key, 6)
    for axis_at, shards_of in cuts:
        steps = jnp.exp(jax.random.uniform(jax.random.fold_in(own, axis_at), (shards_of,), jnp.float32, least / len(cuts), top_value / len(cuts)))
        gain = gain * jnp.repeat(steps, extent[axis_at] // shards_of).reshape([-1 if axis == axis_at else 1 for axis in range(len(extent))])
    return gain


def centred(own_key, shape, scale, bound, cuts=(), kind=jnp.bfloat16):
    gain = level_of(own_key, shape, cuts, -0.22, 0.18) if cuts else 1.0
    result = jax.random.normal(own_key, shape, jnp.float32) * scale * gain
    return jnp.minimum(jnp.maximum(result, -bound), bound).astype(kind)


def setup_inputs(seed: int = 0) -> dict:
    arg_keys = jax.random.split(jax.random.key(seed), 7)
    tokens = centred(arg_keys[0], (TOKENS, D), 1.0, 6.0, ((0, 8),))
    cotangent = centred(arg_keys[1], (TOKENS, FF), 1.0, 6.0, ((0, 2), (1, 16)))
    weight_blocks = centred(arg_keys[2], (SHARDS, CAP, BLK, BLK), (D // 5) ** -0.5, 0.125, ((0, 16),))
    block_rows = draw_block_rows(jax.random.fold_in(arg_keys[6], 71), 0)
    block_cols = draw_block_cols(jax.random.fold_in(arg_keys[6], 71), 0)
    block_count = draw_block_count(jax.random.fold_in(arg_keys[6], 71), 0)
    return dict(tokens=tokens, cotangent=cotangent, weight_blocks=weight_blocks, block_rows=block_rows, block_cols=block_cols, block_count=block_count)


def reference(tokens, cotangent, weight_blocks, block_rows, block_cols, block_count):
    total = tokens.shape[0]
    shards = weight_blocks.shape[0]
    ff_shard = FF // shards
    col_blocks = ff_shard // BLK
    group = total // N_DP
    scale = 1.0 / (total ** 0.5)
    token_blocks = tokens.reshape(total, D // BLK, BLK)

    def one_shard(shard):
        rows = block_rows[shard]
        cols = block_cols[shard]
        live = (jnp.arange(CAP) < block_count[shard]).astype(jnp.float32)
        select = (cols[:, None] == jnp.arange(col_blocks)[None, :]).astype(jnp.float32) * live[:, None]
        blocks = token_blocks[:, rows, :].astype(jnp.float32)
        weights = weight_blocks[shard].astype(jnp.float32)
        product = jnp.einsum('nkb,kbc->nkc', blocks, weights)
        output = jnp.einsum('nkc,kj->njc', product, select).reshape(total, ff_shard).astype(jnp.bfloat16)
        grads = lax.dynamic_slice_in_dim(cotangent, (shard * ff_shard).astype(jnp.int32), ff_shard, 1)
        grads = grads.reshape(total, col_blocks, BLK)[:, cols, :].astype(jnp.float32)
        partial_sums = jnp.einsum('gnkb,gnkc->gkbc', blocks.reshape(N_DP, group, CAP, BLK), grads.reshape(N_DP, group, CAP, BLK))
        partial_sums = (partial_sums * live[None, :, None, None] * scale).astype(jnp.bfloat16)
        summed = jnp.sum(partial_sums.astype(jnp.float32), axis=0).astype(jnp.bfloat16)
        return output, summed

    outputs, grads_all = lax.map(one_shard, jnp.arange(shards, dtype=jnp.int32))
    hidden = jnp.transpose(outputs, (1, 0, 2)).reshape(total, FF)
    return hidden, grads_all
```

```python
import functools

import jax
import jax.numpy as jnp
from jax import lax
from jax.experimental import pallas as pl
from jax.experimental.pallas import tpu as pltpu
from jax.sharding import PartitionSpec as P

ROWS_AT, COLS_AT, UNROLL = 0, 1, 8


def block_kernel(plan, slots, scale, *refs):
    n_tok, n_cot = plan["tokens"], plan["cotangents"]
    table, place = refs[0], refs[1]
    pieces = refs[2 : 2 + n_tok]
    cots = refs[2 + n_tok : 2 + n_tok + n_cot]
    w_hbm = refs[2 + n_tok + n_cot]
    hid_hbm, grad_hbm = refs[3 + n_tok + n_cot : 5 + n_tok + n_cot]
    tok, cot, w, acc, hid, grad, sem_tok, sem_cot, sem_w, sem_out = refs[5 + n_tok + n_cot :]
    capacity, side = w.shape[0], w.shape[1]
    col_blocks, group = acc.shape[0], acc.shape[1]
    parts = sem_w.shape[0]
    per_part = capacity // parts

    w_copies = [
        pltpu.make_async_copy(w_hbm.at[pl.ds(i * per_part, per_part)], w.at[pl.ds(i * per_part, per_part)], sem_w.at[i])
        for i in range(parts)
    ]
    tok_copies = []
    for i, (operand, first, rows, at) in enumerate(plan["pieces"]):
        src = pieces[operand]
        width = src.shape[1]
        row0 = pl.multiple_of(place[2 * at], 16)
        col0 = pl.multiple_of(place[2 * at + 1], side)
        tok_copies.append(
            pltpu.make_async_copy(
                src.at[pl.ds(first, rows)], tok.at[pl.ds(row0, rows), pl.ds(col0, width)], sem_tok.at[i]
            )
        )
    cot_copies = [
        pltpu.make_async_copy(c, cot.at[pl.ds(i * group, group)], sem_cot.at[i]) for i, c in enumerate(cots)
    ]
    for copy in tok_copies + w_copies + cot_copies:
        copy.start()
    acc[...] = jnp.zeros_like(acc)
    count = place[2 * plan["places"]]
    slot0 = place[2 * plan["places"] + 1]
    for copy in tok_copies:
        copy.wait()

    def hidden_step(step, carry):
        base = step * UNROLL
        products = []
        for u in range(UNROLL):
            k = base + u
            lane = pl.multiple_of(table[ROWS_AT, k] * side, side)
            product = jnp.dot(tok[pl.ds(0, group), pl.ds(lane, side)], w[k], preferred_element_type=jnp.float32)
            products.append(jnp.where(k < count, product, 0.0))
        for u in range(UNROLL):
            col = table[COLS_AT, base + u]
            acc[col] = acc[col] + products[u]
        return carry

    for i in range(parts):
        w_copies[i].wait()
        lax.fori_loop(i * per_part // UNROLL, (i + 1) * per_part // UNROLL, hidden_step, 0)
    for j in range(col_blocks):
        hid[:, j * side : (j + 1) * side] = acc[j].astype(hid.dtype)
    out_hid = pltpu.make_async_copy(hid, hid_hbm, sem_out.at[0])
    out_hid.start()
    for copy in cot_copies:
        copy.wait()

    def grad_step(step, carry):
        base = step * UNROLL
        for u in range(UNROLL):
            k = slot0 + base + u
            lane = pl.multiple_of(table[ROWS_AT, k] * side, side)
            col = pl.multiple_of(table[COLS_AT, k] * side, side)
            product = lax.dot_general(
                tok[:, pl.ds(lane, side)],
                cot[:, pl.ds(col, side)],
                (((0,), (0,)), ((), ())),
                preferred_element_type=jnp.float32,
            )
            grad[base + u] = jnp.where(k < count, product * scale, 0.0).astype(grad.dtype)
        return carry

    lax.fori_loop(0, slots // UNROLL, grad_step, 0)
    out_grad = pltpu.make_async_copy(grad, grad_hbm, sem_out.at[1])
    out_grad.start()
    out_hid.wait()
    out_grad.wait()


def run_blocks(table, placements, pieces, plan, cots, weights, count, slot0, slots, scale):
    capacity, side, _ = weights.shape
    group, ff_dev = cots[0].shape
    width = plan["width"]
    flat = [jnp.asarray(v, jnp.int32).reshape(()) for pair in placements for v in pair]
    place = jnp.stack(flat + [count, jnp.asarray(slot0, jnp.int32).reshape(())])
    plan = dict(plan, tokens=len(pieces), cotangents=len(cots), places=len(placements))
    n_any = len(pieces) + len(cots) + 1
    flops = 2 * side * side * group * (capacity + slots * len(cots))
    moved = 2 * (weights.size + slots * side * side + group * len(cots) * (ff_dev + width) + group * ff_dev)
    return pl.pallas_call(
        functools.partial(block_kernel, plan, slots, scale),
        out_shape=(
            jax.ShapeDtypeStruct((group, ff_dev), jnp.bfloat16),
            jax.ShapeDtypeStruct((slots, side, side), jnp.bfloat16),
        ),
        in_specs=[pl.BlockSpec(memory_space=pltpu.SMEM)] * 2 + [pl.BlockSpec(memory_space=pl.ANY)] * n_any,
        out_specs=(pl.BlockSpec(memory_space=pl.ANY),) * 2,
        scratch_shapes=[
            pltpu.VMEM((group * len(cots), width), jnp.bfloat16),
            pltpu.VMEM((group * len(cots), ff_dev), jnp.bfloat16),
            pltpu.VMEM((capacity, side, side), jnp.bfloat16),
            pltpu.VMEM((ff_dev // side, group, side), jnp.float32),
            pltpu.VMEM((group, ff_dev), jnp.bfloat16),
            pltpu.VMEM((slots, side, side), jnp.bfloat16),
            pltpu.SemaphoreType.DMA((len(plan["pieces"]),)),
            pltpu.SemaphoreType.DMA((len(cots),)),
            pltpu.SemaphoreType.DMA((4,)),
            pltpu.SemaphoreType.DMA((2,)),
        ],
        compiler_params=pltpu.CompilerParams(vmem_limit_bytes=40 << 20),
        cost_estimate=pl.CostEstimate(flops=flops, bytes_accessed=moved, transcendentals=0),
        name="blocks",
    )(table, place, *pieces, *cots, weights)


def gather_inputs(tokens, cotangent):
    tok_dev, width = tokens.shape
    quarter = width // 4
    row, col, group = lax.axis_index("row"), lax.axis_index("col"), cotangent.shape[0]
    x, core = col // 2, col % 2
    over_y = functools.partial(lax.ppermute, axis_name="dp", perm=[(0, 1), (1, 0)])
    over_x = functools.partial(lax.ppermute, axis_name="col", perm=[(0, 2), (2, 0), (1, 3), (3, 1)])
    over_core = functools.partial(lax.ppermute, axis_name="col", perm=[(0, 1), (1, 0), (2, 3), (3, 2)])

    def over_z(value, by):
        return lax.ppermute(value, "row", [(i, (i + by) % 4) for i in range(4)])

    mine = lax.dynamic_slice_in_dim(tokens, col * quarter, quarter, 1)
    other = over_y(mine)
    both = jnp.concatenate([mine, other], 0)
    hops = (1, 3, 2)
    arrived = [over_z(both, by) for by in hops]
    other_x = over_x(other)
    arrived_x = [over_x(v) for v in arrived]
    cot_other = over_y(cotangent)

    pieces, placements, listed = [], [], []

    def add(value, first, own, at_row, quarter_x, quarter_core):
        if not pieces or pieces[-1] is not value:
            pieces.append(value)
        row0 = (0 if own else group) + at_row * tok_dev
        listed.append((len(pieces) - 1, first, tok_dev, len(placements)))
        placements.append((row0, (quarter_x * 2 + quarter_core) * quarter))

    pieces.append(tokens)
    listed.append((0, 0, tok_dev, 0))
    placements.append((row * tok_dev, 0))
    for value, quarter_x in ((other, x), (other_x, 1 - x)):
        add(value, 0, False, row, quarter_x, core)
        add(over_core(value), 0, False, row, quarter_x, 1 - core)
    for values, quarter_x in ((arrived, x), (arrived_x, 1 - x)):
        for by, value in zip(hops, values):
            at_row = (row + 4 - by) % 4
            for sent, quarter_core in ((value, core), (over_core(value), 1 - core)):
                add(sent, 0, True, at_row, quarter_x, quarter_core)
                add(sent, tok_dev, False, at_row, quarter_x, quarter_core)
    return pieces, placements, listed, [cotangent, cot_other]


def on_device(tokens, cotangent, weight_blocks, block_rows, block_cols, block_count):
    groups, steps = lax.axis_size("dp"), lax.axis_size("row")
    tok_dev, width = tokens.shape
    group = cotangent.shape[0]
    weights = weight_blocks[0]
    capacity = weights.shape[0]
    scale = 1.0 / (group * groups) ** 0.5
    table = jnp.concatenate([block_rows, block_cols], 0)
    count = block_count[0]
    if (groups, steps, lax.axis_size("col")) == (2, 4, 4):
        slots = capacity // groups
        pieces, placements, listed, cots = gather_inputs(tokens, cotangent)
        plan = {"pieces": listed, "width": width}
        slot0 = lax.axis_index("dp") * slots
        hidden, grad = run_blocks(table, placements, pieces, plan, cots, weights, count, slot0, slots, scale)
        return hidden, grad[None]
    gathered = lax.all_gather(tokens, "row", axis=0, tiled=True)
    plan = {"pieces": [(0, 0, group, 0)], "width": width}
    hidden, partial = run_blocks(table, [(0, 0)], [gathered], plan, [cotangent], weights, count, 0, capacity, scale)
    return hidden, lax.psum_scatter(partial[None], "dp", scatter_dimension=1, tiled=True)


def solution(mesh):
    in_specs = (
        P(("dp", "row"), None),
        P("dp", ("row", "col")),
        P(("row", "col"), None, None, None),
        P(("row", "col"), None),
        P(("row", "col"), None),
        P(("row", "col")),
    )
    out_specs = (P("dp", ("row", "col")), P(("row", "col"), "dp", None, None))
    return jax.shard_map(
        on_device, mesh=mesh, in_specs=in_specs, out_specs=out_specs, check_vma=False
    )
```

```python
import functools

import jax
import jax.numpy as jnp
from jax import lax
from jax.experimental import pallas as pl
from jax.experimental.pallas import tpu as pltpu
from jax.sharding import PartitionSpec as P

UNROLL = 24
OUT_PARTS = 2
VMEM_LIMIT = 40 << 20


def assemble(place, pieces, plan, tok):
    for operand, first, rows, row0, at in plan:
        src = pieces[operand]
        if at is None:
            tok[row0 : row0 + rows, :] = src[first : first + rows, :]
        else:
            lane = pl.multiple_of(place[at], 128)
            tok[row0 : row0 + rows, pl.ds(lane, src.shape[1])] = src[first : first + rows, :]


def hidden_kernel(plan, n, shard, table, place, *refs):
    pieces, w, hid_hbm = refs[:n], refs[n], refs[n + 1]
    tok, acc, hid, sem_out = refs[n + 2 :]
    capacity, side = w.shape[0], w.shape[1]
    col_blocks, group = acc.shape[0], acc.shape[1]
    acc[...] = jnp.zeros_like(acc)
    assemble(place, pieces, plan, tok)
    live = place[place.shape[0] - 2]

    def step_of(step, carry):
        base = step * UNROLL
        products = []
        for u in range(UNROLL):
            k = base + u
            lane = pl.multiple_of(table[0, k] * side, side)
            product = jnp.dot(tok[:, pl.ds(lane, side)], w[k], preferred_element_type=jnp.float32)
            products.append(jnp.where(k < live, product, 0.0))
        for u in range(UNROLL):
            col = table[1, base + u]
            acc[col] = acc[col] + products[u]
        return carry

    lax.fori_loop(0, capacity // UNROLL, step_of, 0)
    for j in range(col_blocks):
        for i in range(group // shard):
            row0 = pl.multiple_of(place[i], 16)
            hid[pl.ds(row0, shard), j * side : (j + 1) * side] = acc[j, i * shard : (i + 1) * shard, :].astype(hid.dtype)
    out = pltpu.make_async_copy(hid, hid_hbm, sem_out.at[0])
    out.start()
    out.wait()


def grad_kernel(plan, n, shard, scale, table, place, *refs):
    pieces = refs[:n]
    n_cot = (len(refs) - n - 5)
    cots, grad_hbm = refs[n : n + n_cot], refs[n + n_cot]
    tok, cot, grad, sem_out = refs[n + n_cot + 1 :]
    slots, side = grad.shape[0], grad.shape[1]
    group = cots[0].shape[0]
    assemble(place, pieces, plan, tok)
    for g, src in enumerate(cots):
        for i in range(group // shard):
            row0 = pl.multiple_of(place[i], 16)
            at = g * group + i * shard
            cot[at : at + shard, :] = src[pl.ds(row0, shard), :]
    live = place[place.shape[0] - 2]
    slot0 = place[place.shape[0] - 1]

    def step_of(step, carry):
        base = step * UNROLL
        for u in range(UNROLL):
            k = slot0 + base + u
            lane = pl.multiple_of(table[0, k] * side, side)
            col = pl.multiple_of(table[1, k] * side, side)
            product = lax.dot_general(
                tok[:, pl.ds(lane, side)],
                cot[:, pl.ds(col, side)],
                (((0,), (0,)), ((), ())),
                preferred_element_type=jnp.float32,
            )
            grad[base + u] = jnp.where(k < live, product * scale, 0.0).astype(grad.dtype)
        return carry

    per_part = slots // OUT_PARTS
    copies = []
    for i in range(OUT_PARTS):
        lax.fori_loop(i * per_part // UNROLL, (i + 1) * per_part // UNROLL, step_of, 0)
        part = pl.ds(i * per_part, per_part)
        copies.append(pltpu.make_async_copy(grad.at[part], grad_hbm.at[part], sem_out.at[i]))
        copies[-1].start()
    for copy in copies:
        copy.wait()


def call_hidden(table, place, pieces, plan, weights, group, ff_dev, width, shard):
    capacity, side, _ = weights.shape
    cost = pl.CostEstimate(
        flops=2 * side * side * group * capacity,
        bytes_accessed=2 * (weights.size + group * (width + ff_dev)),
        transcendentals=0,
    )
    return pl.pallas_call(
        functools.partial(hidden_kernel, plan, len(pieces), shard),
        out_shape=jax.ShapeDtypeStruct((group, ff_dev), jnp.bfloat16),
        in_specs=[pl.BlockSpec(memory_space=pltpu.SMEM)] * 2
        + [pl.BlockSpec(memory_space=pltpu.VMEM)] * len(pieces)
        + [pl.BlockSpec(memory_space=pltpu.VMEM)],
        out_specs=pl.BlockSpec(memory_space=pltpu.HBM),
        scratch_shapes=[
            pltpu.VMEM((group, width), jnp.bfloat16),
            pltpu.VMEM((ff_dev // side, group, side), jnp.float32),
            pltpu.VMEM((group, ff_dev), jnp.bfloat16),
            pltpu.SemaphoreType.DMA((1,)),
        ],
        compiler_params=pltpu.CompilerParams(vmem_limit_bytes=VMEM_LIMIT),
        cost_estimate=cost,
        name="hidden",
    )(table, place, *pieces, weights)


def call_grad(table, place, pieces, plan, cots, slots, side, width, shard, scale):
    group, ff_dev = cots[0].shape
    total = group * len(cots)
    cost = pl.CostEstimate(
        flops=2 * side * side * total * slots,
        bytes_accessed=2 * (slots * side * side + total * (width + ff_dev)),
        transcendentals=0,
    )
    return pl.pallas_call(
        functools.partial(grad_kernel, plan, len(pieces), shard, scale),
        out_shape=jax.ShapeDtypeStruct((slots, side, side), jnp.bfloat16),
        in_specs=[pl.BlockSpec(memory_space=pltpu.SMEM)] * 2
        + [pl.BlockSpec(memory_space=pltpu.VMEM)] * (len(pieces) + len(cots)),
        out_specs=pl.BlockSpec(memory_space=pltpu.HBM),
        scratch_shapes=[
            pltpu.VMEM((total, width), jnp.bfloat16),
            pltpu.VMEM((total, ff_dev), jnp.bfloat16),
            pltpu.VMEM((slots, side, side), jnp.bfloat16),
            pltpu.SemaphoreType.DMA((OUT_PARTS,)),
        ],
        compiler_params=pltpu.CompilerParams(vmem_limit_bytes=VMEM_LIMIT),
        cost_estimate=cost,
        name="grad",
    )(table, place, *pieces, *cots)


def two_group_plan(table, count, tokens, cotangent, weights, scale):
    tok_dev, width = tokens.shape
    quarter = width // 4
    group, ff_dev = cotangent.shape
    capacity, side, _ = weights.shape
    slots = capacity // 2
    row, col = lax.axis_index("row"), lax.axis_index("col")
    x, core = col // 2, col % 2
    swap_y = functools.partial(lax.ppermute, axis_name="dp", perm=[(0, 1), (1, 0)])

    def over_y(bundle):
        value, parts = bundle
        return swap_y(value), [(not own, shard, at) for own, shard, at in parts]

    def over_x(bundle):
        value, parts = bundle
        moved = lax.ppermute(value, "col", [(0, 2), (2, 0), (1, 3), (3, 1)])
        return moved, [(own, shard, at ^ 1) for own, shard, at in parts]

    def over_core(bundle):
        value, parts = bundle
        moved = lax.ppermute(value, "col", [(0, 1), (1, 0), (2, 3), (3, 2)])
        return moved, [(own, shard, at ^ 2) for own, shard, at in parts]

    def over_z(bundle, shard):
        value, parts = bundle
        by = (0, 1, 3, 2)[shard]
        moved = lax.ppermute(value, "row", [(i, (i + by) % 4) for i in range(4)])
        return moved, [(own, shard, at) for own, _, at in parts]

    def join(*bundles):
        return jnp.concatenate([v for v, _ in bundles], 0), [p for _, parts in bundles for p in parts]

    def cut(bundle, i, j):
        return bundle[0][i * tok_dev : j * tok_dev], bundle[1][i:j]

    def after(bundle, *earlier):
        return lax.optimization_barrier((bundle[0], [e[0] for e in earlier]))[0], bundle[1]

    place = [((row + 4 - by) % 4) * tok_dev for by in (0, 1, 3, 2)]
    place += [(xx * 2 + cc) * quarter for xx, cc in ((x, core), (1 - x, core), (x, 1 - core), (1 - x, 1 - core))]
    place = jnp.stack(place + [count, lax.axis_index("dp") * slots]).astype(jnp.int32)
    mine = lax.dynamic_slice_in_dim(tokens, col * quarter, quarter, 1)

    def planned(bundles, pick):
        pieces, plan = [tokens], [(0, 0, tok_dev, 0, None)]
        for value, parts in bundles:
            if any(map(pick, parts)):
                for i, (own, shard, at) in enumerate(parts):
                    if pick((own, shard, at)):
                        plan.append((len(pieces), i * tok_dev, tok_dev, (0 if own else group) + shard * tok_dev, 4 + at))
                pieces.append(value)
        return pieces, plan

    def run_hidden(*bundles):
        pieces, plan = planned(bundles, lambda part: part[0])
        assert len(plan) == 13
        return call_hidden(table, place, pieces, plan, weights, group, ff_dev, width, tok_dev)

    mine = (mine, [(True, 0, 0)])
    other0 = over_y(mine)
    own3 = over_z(mine, 3)
    both = join(mine, other0)
    both1 = over_z(both, 1)
    both2 = over_z(both, 2)
    other3 = over_y(own3)
    cot_other = swap_y(after((cotangent, None), other3)[0])
    own2, other2 = cut(both2, 0, 1), cut(both2, 1, 2)
    first = join(own3, other0)
    first_x = over_x(first)
    both1_x = over_x(both1)
    own2_x = over_x(own2)
    last = join(other3, other2)
    last_x = over_x(last)
    settled, (table, place) = lax.optimization_barrier((join(first, both1)[0], (table, place)))
    core_a = over_core((settled, join(first, both1)[1]))
    core_b = over_core(join(first_x, both1_x, own2, own2_x))
    hidden = run_hidden(first, both1, own2, first_x, both1_x, own2_x, core_a, core_b)
    core_c = over_core(join(last, last_x))
    got = [first, both1, own2, first_x, both1_x, own2_x, core_a, core_b, last, last_x, core_c]
    pieces, plan = planned(got, lambda part: True)
    assert len(plan) == 29
    grad = call_grad(table, place, pieces, plan, [cotangent, cot_other], slots, side, width, tok_dev, scale)
    return hidden, grad


def on_device(tokens, cotangent, weight_blocks, block_rows, block_cols, block_count):
    groups, steps = lax.axis_size("dp"), lax.axis_size("row")
    tok_dev, width = tokens.shape
    group, ff_dev = cotangent.shape
    weights = weight_blocks[0]
    capacity, side, _ = weights.shape
    scale = 1.0 / (group * groups) ** 0.5
    table, count = jnp.concatenate([block_rows, block_cols], 0), block_count[0]
    if (groups, steps, lax.axis_size("col")) == (2, 4, 4):
        hidden, grad = two_group_plan(table, count, tokens, cotangent, weights, scale)
        return hidden, grad[None]
    gathered = lax.all_gather(tokens, "row", axis=0, tiled=True)
    zero = jnp.zeros((), jnp.int32)
    place = jnp.stack([zero, count, zero])
    plan = [(0, 0, group, 0, None)]
    hidden = call_hidden(table, place, [gathered], plan, weights, group, ff_dev, width, group)
    partial = call_grad(table, place, [gathered], plan, [cotangent], capacity, side, width, group, scale)
    return hidden, lax.psum_scatter(partial[None], "dp", scatter_dimension=1, tiled=True)


def solution(mesh):
    in_specs = (
        P(("dp", "row"), None),
        P("dp", ("row", "col")),
        P(("row", "col"), None, None, None),
        P(("row", "col"), None),
        P(("row", "col"), None),
        P(("row", "col")),
    )
    out_specs = (P("dp", ("row", "col")), P(("row", "col"), "dp", None, None))
    return jax.shard_map(
        on_device, mesh=mesh, in_specs=in_specs, out_specs=out_specs, check_vma=False
    )
```

```python
import functools

import jax
import jax.numpy as jnp
from jax import lax
from jax.experimental import pallas as pl
from jax.experimental.pallas import tpu as pltpu
from jax.sharding import PartitionSpec as P

UNROLL = 24
OUT_PARTS = 2
VMEM_LIMIT = 24 << 20


def block_kernel(plan, n_pieces, n_cots, shard, scale, table, place, *refs):
    pieces, cots = refs[:n_pieces], refs[n_pieces : n_pieces + n_cots]
    w, hid_hbm, grad_hbm, tok, cot, acc, hid, grad, sem = refs[n_pieces + n_cots :]
    capacity, side = w.shape[0], w.shape[1]
    col_blocks, group = acc.shape[0], acc.shape[1]
    slots = grad.shape[0]
    live, slot0 = place[place.shape[0] - 2], place[place.shape[0] - 1]
    acc[...] = jnp.zeros_like(acc)
    for operand, first, rows, row0, at in plan:
        src = pieces[operand]
        if at is None:
            tok[row0 : row0 + rows, :] = src[first : first + rows, :]
        else:
            lane = pl.multiple_of(place[at], 128)
            tok[row0 : row0 + rows, pl.ds(lane, src.shape[1])] = src[first : first + rows, :]
    for g, src in enumerate(cots):
        for i in range(group // shard):
            at = g * group + i * shard
            cot[at : at + shard, :] = src[pl.ds(pl.multiple_of(place[i], 16), shard), :]

    def grad_step(step, carry):
        base = step * UNROLL
        for u in range(UNROLL):
            k = slot0 + base + u
            lane = pl.multiple_of(table[0, k] * side, side)
            col = pl.multiple_of(table[1, k] * side, side)
            product = lax.dot_general(
                tok[:, pl.ds(lane, side)],
                cot[:, pl.ds(col, side)],
                (((0,), (0,)), ((), ())),
                preferred_element_type=jnp.float32,
            )
            grad[base + u] = jnp.where(k < live, product * scale, 0.0).astype(grad.dtype)
        return carry

    def hidden_step(step, carry):
        base = step * UNROLL
        products = []
        for u in range(UNROLL):
            k = base + u
            lane = pl.multiple_of(table[0, k] * side, side)
            product = jnp.dot(tok[0:group, pl.ds(lane, side)], w[k], preferred_element_type=jnp.float32)
            products.append(jnp.where(k < live, product, 0.0))
        for u in range(UNROLL):
            col = table[1, base + u]
            acc[col] = acc[col] + products[u]
        return carry

    per_part = slots // OUT_PARTS
    copies = []
    for i in range(OUT_PARTS):
        lax.fori_loop(i * per_part // UNROLL, (i + 1) * per_part // UNROLL, grad_step, 0)
        part = pl.ds(i * per_part, per_part)
        copies.append(pltpu.make_async_copy(grad.at[part], grad_hbm.at[part], sem.at[i]))
        copies[-1].start()
    lax.fori_loop(0, capacity // UNROLL, hidden_step, 0)
    for j in range(col_blocks):
        for i in range(group // shard):
            row0 = pl.multiple_of(place[i], 16)
            hid[pl.ds(row0, shard), j * side : (j + 1) * side] = acc[j, i * shard : (i + 1) * shard, :].astype(hid.dtype)
    copies.append(pltpu.make_async_copy(hid, hid_hbm, sem.at[OUT_PARTS]))
    copies[-1].start()
    for copy in copies:
        copy.wait()


def call_blocks(table, place, pieces, plan, weights, cots, slots, width, shard, scale):
    capacity, side, _ = weights.shape
    group, ff_dev = cots[0].shape
    total = group * len(cots)
    cost = pl.CostEstimate(
        flops=2 * side * side * (group * capacity + total * slots),
        bytes_accessed=2 * (weights.size + slots * side * side + total * (width + ff_dev) + group * ff_dev),
        transcendentals=0,
    )
    return pl.pallas_call(
        functools.partial(block_kernel, plan, len(pieces), len(cots), shard, scale),
        out_shape=(
            jax.ShapeDtypeStruct((group, ff_dev), jnp.bfloat16),
            jax.ShapeDtypeStruct((slots, side, side), jnp.bfloat16),
        ),
        in_specs=[pl.BlockSpec(memory_space=pltpu.SMEM)] * 2
        + [pl.BlockSpec(memory_space=pltpu.VMEM)] * (len(pieces) + len(cots) + 1),
        out_specs=(pl.BlockSpec(memory_space=pltpu.HBM),) * 2,
        scratch_shapes=[
            pltpu.VMEM((total, width), jnp.bfloat16),
            pltpu.VMEM((total, ff_dev), jnp.bfloat16),
            pltpu.VMEM((ff_dev // side, group, side), jnp.float32),
            pltpu.VMEM((group, ff_dev), jnp.bfloat16),
            pltpu.VMEM((slots, side, side), jnp.bfloat16),
            pltpu.SemaphoreType.DMA((OUT_PARTS + 1,)),
        ],
        compiler_params=pltpu.CompilerParams(vmem_limit_bytes=VMEM_LIMIT),
        cost_estimate=cost,
        name="blocks",
    )(table, place, *pieces, *cots, weights)


def two_group_plan(table, count, tokens, cotangent, weights, scale):
    tok_dev, width = tokens.shape
    quarter = width // 4
    group, ff_dev = cotangent.shape
    capacity, side, _ = weights.shape
    slots = capacity // 2
    row, col = lax.axis_index("row"), lax.axis_index("col")
    x, core = col // 2, col % 2
    swap_y = functools.partial(lax.ppermute, axis_name="dp", perm=[(0, 1), (1, 0)])

    def over_y(bundle):
        value, parts = bundle
        return swap_y(value), [(not own, shard, at) for own, shard, at in parts]

    def over_x(bundle):
        value, parts = bundle
        moved = lax.ppermute(value, "col", [(0, 2), (2, 0), (1, 3), (3, 1)])
        return moved, [(own, shard, at ^ 1) for own, shard, at in parts]

    def over_core(bundle):
        value, parts = bundle
        moved = lax.ppermute(value, "col", [(0, 1), (1, 0), (2, 3), (3, 2)])
        return moved, [(own, shard, at ^ 2) for own, shard, at in parts]

    def over_z(bundle, shard):
        value, parts = bundle
        by = (0, 1, 3, 2)[shard]
        moved = lax.ppermute(value, "row", [(i, (i + by) % 4) for i in range(4)])
        return moved, [(own, shard, at) for own, _, at in parts]

    def join(*bundles):
        return jnp.concatenate([v for v, _ in bundles], 0), [p for _, parts in bundles for p in parts]

    def cut(bundle, i, j):
        return bundle[0][i * tok_dev : j * tok_dev], bundle[1][i:j]

    def after(bundle, *earlier):
        return lax.optimization_barrier((bundle[0], [e[0] for e in earlier]))[0], bundle[1]

    place = [((row + 4 - by) % 4) * tok_dev for by in (0, 1, 3, 2)]
    place += [(xx * 2 + cc) * quarter for xx, cc in ((x, core), (1 - x, core), (x, 1 - core), (1 - x, 1 - core))]
    place = jnp.stack(place + [count, lax.axis_index("dp") * slots]).astype(jnp.int32)
    mine = lax.dynamic_slice_in_dim(tokens, col * quarter, quarter, 1)

    mine = (mine, [(True, 0, 0)])
    other0 = over_y(mine)
    own3 = over_z(mine, 3)
    both = join(mine, other0)
    both1 = over_z(both, 1)
    both2 = over_z(both, 2)
    other3 = over_y(own3)
    cot_other = swap_y(after((cotangent, None), other3)[0])
    own2, other2 = cut(both2, 0, 1), cut(both2, 1, 2)
    first = join(own3, other0)
    first_x = over_x(first)
    both1_x = over_x(both1)
    own2_x = over_x(own2)
    last = join(other3, other2)
    last_x = over_x(after(last, both1))
    near = join(first, both1)
    settled, (table, place) = lax.optimization_barrier((near[0], (table, place)))
    core_a = over_core((settled, near[1]))
    core_b = over_core(join(first_x, both1_x, own2, own2_x))
    core_c = over_core(join(last, last_x))
    got = [first, both1, own2, first_x, both1_x, own2_x, core_a, core_b, last, last_x, core_c]
    pieces, plan = [tokens], [(0, 0, tok_dev, 0, None)]
    for value, parts in got:
        for i, (own, shard, at) in enumerate(parts):
            plan.append((len(pieces), i * tok_dev, tok_dev, (0 if own else group) + shard * tok_dev, 4 + at))
        pieces.append(value)
    assert len(plan) == 29
    return call_blocks(
        table, place, pieces, plan, weights, [cotangent, cot_other], slots, width, tok_dev, scale
    )


def on_device(tokens, cotangent, weight_blocks, block_rows, block_cols, block_count):
    groups, steps = lax.axis_size("dp"), lax.axis_size("row")
    tok_dev, width = tokens.shape
    group, ff_dev = cotangent.shape
    weights = weight_blocks[0]
    capacity, side, _ = weights.shape
    scale = 1.0 / (group * groups) ** 0.5
    table, count = jnp.concatenate([block_rows, block_cols], 0), block_count[0]
    if (groups, steps, lax.axis_size("col")) == (2, 4, 4):
        hidden, grad = two_group_plan(table, count, tokens, cotangent, weights, scale)
        return hidden, grad[None]
    gathered = lax.all_gather(tokens, "row", axis=0, tiled=True)
    zero = jnp.zeros((), jnp.int32)
    place = jnp.stack([zero, count, zero])
    plan = [(0, 0, group, 0, None)]
    hidden, partial = call_blocks(table, place, [gathered], plan, weights, [cotangent], capacity, width, group, scale)
    return hidden, lax.psum_scatter(partial[None], "dp", scatter_dimension=1, tiled=True)


def solution(mesh):
    in_specs = (
        P(("dp", "row"), None),
        P("dp", ("row", "col")),
        P(("row", "col"), None, None, None),
        P(("row", "col"), None),
        P(("row", "col"), None),
        P(("row", "col")),
    )
    out_specs = (P("dp", ("row", "col")), P(("row", "col"), "dp", None, None))
    return jax.shard_map(
        on_device, mesh=mesh, in_specs=in_specs, out_specs=out_specs, check_vma=False
    )
```

```python
import functools

import jax
import jax.numpy as jnp
from jax import lax
from jax.experimental import pallas as pl
from jax.experimental.pallas import tpu as pltpu
from jax.sharding import PartitionSpec as P

UNROLL = 48
OUT_PARTS = 1
VMEM_LIMIT = 24 << 20


def block_kernel(plan, n_pieces, n_cots, shard, scale, table, place, *refs):
    pieces, cots = refs[:n_pieces], refs[n_pieces : n_pieces + n_cots]
    w, hid_hbm, grad_hbm, tok, cot, acc, hid, grad, sem = refs[n_pieces + n_cots :]
    capacity, side = w.shape[0], w.shape[1]
    col_blocks, group = acc.shape[0], acc.shape[1]
    slots = grad.shape[0]
    live, slot0 = place[place.shape[0] - 2], place[place.shape[0] - 1]
    acc[...] = jnp.zeros_like(acc)
    for operand, first, rows, row0, at in plan:
        src = pieces[operand]
        if at is None:
            tok[row0 : row0 + rows, :] = src[first : first + rows, :]
        else:
            lane = pl.multiple_of(place[at], 128)
            tok[row0 : row0 + rows, pl.ds(lane, src.shape[1])] = src[first : first + rows, :]
    for g, src in enumerate(cots):
        for i in range(group // shard):
            at = g * group + i * shard
            cot[at : at + shard, :] = src[pl.ds(pl.multiple_of(place[i], 16), shard), :]

    def grad_step(step, carry):
        base = step * UNROLL
        for u in range(UNROLL):
            k = slot0 + base + u
            lane = pl.multiple_of(table[0, k] * side, side)
            col = pl.multiple_of(table[1, k] * side, side)
            product = lax.dot_general(
                tok[:, pl.ds(lane, side)],
                cot[:, pl.ds(col, side)],
                (((0,), (0,)), ((), ())),
                preferred_element_type=jnp.float32,
            )
            grad[base + u] = jnp.where(k < live, product * scale, 0.0).astype(grad.dtype)
        return carry

    def hidden_step(step, carry):
        base = step * UNROLL
        products = []
        for u in range(UNROLL):
            k = base + u
            lane = pl.multiple_of(table[0, k] * side, side)
            product = jnp.dot(tok[0:group, pl.ds(lane, side)], w[k], preferred_element_type=jnp.float32)
            products.append(jnp.where(k < live, product, 0.0))
        for u in range(UNROLL):
            col = table[1, base + u]
            acc[col] = acc[col] + products[u]
        return carry

    per_part = slots // OUT_PARTS
    copies = []
    for i in range(OUT_PARTS):
        lax.fori_loop(i * per_part // UNROLL, (i + 1) * per_part // UNROLL, grad_step, 0)
        part = pl.ds(i * per_part, per_part)
        copies.append(pltpu.make_async_copy(grad.at[part], grad_hbm.at[part], sem.at[i]))
        copies[-1].start()
    lax.fori_loop(0, capacity // UNROLL, hidden_step, 0)
    for j in range(col_blocks):
        for i in range(group // shard):
            row0 = pl.multiple_of(place[i], 16)
            hid[pl.ds(row0, shard), j * side : (j + 1) * side] = acc[j, i * shard : (i + 1) * shard, :].astype(hid.dtype)
    copies.append(pltpu.make_async_copy(hid, hid_hbm, sem.at[OUT_PARTS]))
    copies[-1].start()
    for copy in copies:
        copy.wait()


def call_blocks(table, place, pieces, plan, weights, cots, slots, width, shard, scale):
    capacity, side, _ = weights.shape
    group, ff_dev = cots[0].shape
    total = group * len(cots)
    cost = pl.CostEstimate(
        flops=2 * side * side * (group * capacity + total * slots),
        bytes_accessed=2 * (weights.size + slots * side * side + total * (width + ff_dev) + group * ff_dev),
        transcendentals=0,
    )
    return pl.pallas_call(
        functools.partial(block_kernel, plan, len(pieces), len(cots), shard, scale),
        out_shape=(
            jax.ShapeDtypeStruct((group, ff_dev), jnp.bfloat16),
            jax.ShapeDtypeStruct((slots, side, side), jnp.bfloat16),
        ),
        in_specs=[pl.BlockSpec(memory_space=pltpu.SMEM)] * 2
        + [pl.BlockSpec(memory_space=pltpu.VMEM)] * (len(pieces) + len(cots) + 1),
        out_specs=(pl.BlockSpec(memory_space=pltpu.HBM),) * 2,
        scratch_shapes=[
            pltpu.VMEM((total, width), jnp.bfloat16),
            pltpu.VMEM((total, ff_dev), jnp.bfloat16),
            pltpu.VMEM((ff_dev // side, group, side), jnp.float32),
            pltpu.VMEM((group, ff_dev), jnp.bfloat16),
            pltpu.VMEM((slots, side, side), jnp.bfloat16),
            pltpu.SemaphoreType.DMA((OUT_PARTS + 1,)),
        ],
        compiler_params=pltpu.CompilerParams(vmem_limit_bytes=VMEM_LIMIT),
        cost_estimate=cost,
        name="blocks",
    )(table, place, *pieces, *cots, weights)


def two_group_plan(table, count, tokens, cotangent, weights, scale):
    tok_dev, width = tokens.shape
    quarter = width // 4
    group, ff_dev = cotangent.shape
    capacity, side, _ = weights.shape
    slots = capacity // 2
    row, col = lax.axis_index("row"), lax.axis_index("col")
    x, core = col // 2, col % 2
    swap_y = functools.partial(lax.ppermute, axis_name="dp", perm=[(0, 1), (1, 0)])

    def over_y(bundle):
        value, parts = bundle
        return swap_y(value), [(not own, shard, at) for own, shard, at in parts]

    def over_x(bundle):
        value, parts = bundle
        moved = lax.ppermute(value, "col", [(0, 2), (2, 0), (1, 3), (3, 1)])
        return moved, [(own, shard, at ^ 1) for own, shard, at in parts]

    def over_core(bundle):
        value, parts = bundle
        moved = lax.ppermute(value, "col", [(0, 1), (1, 0), (2, 3), (3, 2)])
        return moved, [(own, shard, at ^ 2) for own, shard, at in parts]

    def over_z(bundle, shard):
        value, parts = bundle
        by = (0, 1, 3, 2)[shard]
        moved = lax.ppermute(value, "row", [(i, (i + by) % 4) for i in range(4)])
        return moved, [(own, shard, at) for own, _, at in parts]

    def join(*bundles):
        return jnp.concatenate([v for v, _ in bundles], 0), [p for _, parts in bundles for p in parts]

    def cut(bundle, i, j):
        return bundle[0][i * tok_dev : j * tok_dev], bundle[1][i:j]

    def after(bundle, *earlier):
        return lax.optimization_barrier((bundle[0], [e[0] for e in earlier]))[0], bundle[1]

    place = [((row + 4 - by) % 4) * tok_dev for by in (0, 1, 3, 2)]
    place += [(xx * 2 + cc) * quarter for xx, cc in ((x, core), (1 - x, core), (x, 1 - core), (1 - x, 1 - core))]
    place = jnp.stack(place + [count, lax.axis_index("dp") * slots]).astype(jnp.int32)
    mine = lax.dynamic_slice_in_dim(tokens, col * quarter, quarter, 1)

    mine = (mine, [(True, 0, 0)])
    other0 = over_y(mine)
    own3 = over_z(mine, 3)
    both = join(mine, other0)
    both1 = over_z(both, 1)
    both2 = over_z(both, 2)
    other3 = over_y(own3)
    cot_other = swap_y(after((cotangent, None), other3)[0])
    own2, other2 = cut(both2, 0, 1), cut(both2, 1, 2)
    first = join(own3, other0)
    first_x = over_x(first)
    both1_x = over_x(both1)
    own2_x = over_x(own2)
    last = join(other3, other2)
    other2_x = over_x(after(other2, both1))
    other3_x = over_y(after(cut(first_x, 0, 1), both1, own2_x))
    near = join(first, both1)
    settled, (table, place) = lax.optimization_barrier((near[0], (table, place)))
    core_a = over_core((settled, near[1]))
    core_b = over_core(join(first_x, both1_x, own2, own2_x))
    core_c = over_core(join(last, other2_x, other3_x))
    got = [first, both1, own2, first_x, both1_x, own2_x, core_a, core_b, last, other2_x, other3_x, core_c]
    pieces, plan = [tokens], [(0, 0, tok_dev, 0, None)]
    for value, parts in got:
        for i, (own, shard, at) in enumerate(parts):
            plan.append((len(pieces), i * tok_dev, tok_dev, (0 if own else group) + shard * tok_dev, 4 + at))
        pieces.append(value)
    assert len(plan) == 29
    return call_blocks(
        table, place, pieces, plan, weights, [cotangent, cot_other], slots, width, tok_dev, scale
    )


def on_device(tokens, cotangent, weight_blocks, block_rows, block_cols, block_count):
    groups, steps = lax.axis_size("dp"), lax.axis_size("row")
    tok_dev, width = tokens.shape
    group, ff_dev = cotangent.shape
    weights = weight_blocks[0]
    capacity, side, _ = weights.shape
    scale = 1.0 / (group * groups) ** 0.5
    table, count = jnp.concatenate([block_rows, block_cols], 0), block_count[0]
    if (groups, steps, lax.axis_size("col")) == (2, 4, 4):
        hidden, grad = two_group_plan(table, count, tokens, cotangent, weights, scale)
        return hidden, grad[None]
    gathered = lax.all_gather(tokens, "row", axis=0, tiled=True)
    zero = jnp.zeros((), jnp.int32)
    place = jnp.stack([zero, count, zero])
    plan = [(0, 0, group, 0, None)]
    hidden, partial = call_blocks(table, place, [gathered], plan, weights, [cotangent], capacity, width, group, scale)
    return hidden, lax.psum_scatter(partial[None], "dp", scatter_dimension=1, tiled=True)


def solution(mesh):
    in_specs = (
        P(("dp", "row"), None),
        P("dp", ("row", "col")),
        P(("row", "col"), None, None, None),
        P(("row", "col"), None),
        P(("row", "col"), None),
        P(("row", "col")),
    )
    out_specs = (P("dp", ("row", "col")), P(("row", "col"), "dp", None, None))
    return jax.shard_map(
        on_device, mesh=mesh, in_specs=in_specs, out_specs=out_specs, check_vma=False
    )
```

```python
import functools

import jax
import jax.numpy as jnp
from jax import lax
from jax.experimental import pallas as pl
from jax.experimental.pallas import tpu as pltpu
from jax.sharding import PartitionSpec as P

UNROLL = 48
OUT_PARTS = 1
VMEM_LIMIT = 24 << 20


def block_kernel(plan, n_pieces, n_cots, shard, scale, table, place, *refs):
    pieces, cots = refs[:n_pieces], refs[n_pieces : n_pieces + n_cots]
    w, hid_hbm, grad_hbm, tok, cot, acc, hid, grad, sem = refs[n_pieces + n_cots :]
    capacity, side = w.shape[0], w.shape[1]
    col_blocks, group = acc.shape[0], acc.shape[1]
    slots = grad.shape[0]
    live, slot0 = place[place.shape[0] - 2], place[place.shape[0] - 1]
    acc[...] = jnp.zeros_like(acc)
    for operand, first, rows, row0, at in plan:
        src = pieces[operand]
        if at is None:
            tok[row0 : row0 + rows, :] = src[first : first + rows, :]
        else:
            lane = pl.multiple_of(place[at], 128)
            tok[row0 : row0 + rows, pl.ds(lane, src.shape[1])] = src[first : first + rows, :]
    for g, src in enumerate(cots):
        for i in range(group // shard):
            at = g * group + i * shard
            cot[at : at + shard, :] = src[pl.ds(pl.multiple_of(place[i], 16), shard), :]

    def grad_step(step, carry):
        base = step * UNROLL
        for u in range(UNROLL):
            k = slot0 + base + u
            lane = pl.multiple_of(table[0, k] * side, side)
            col = pl.multiple_of(table[1, k] * side, side)
            product = lax.dot_general(
                tok[:, pl.ds(lane, side)],
                cot[:, pl.ds(col, side)],
                (((0,), (0,)), ((), ())),
                preferred_element_type=jnp.float32,
            )
            grad[base + u] = jnp.where(k < live, product * scale, 0.0).astype(grad.dtype)
        return carry

    def hidden_step(step, carry):
        base = step * UNROLL
        products = []
        for u in range(UNROLL):
            k = base + u
            lane = pl.multiple_of(table[0, k] * side, side)
            product = jnp.dot(tok[0:group, pl.ds(lane, side)], w[k], preferred_element_type=jnp.float32)
            products.append(jnp.where(k < live, product, 0.0))
        for u in range(UNROLL):
            col = table[1, base + u]
            acc[col] = acc[col] + products[u]
        return carry

    per_part = slots // OUT_PARTS
    copies = []
    for i in range(OUT_PARTS):
        lax.fori_loop(i * per_part // UNROLL, (i + 1) * per_part // UNROLL, grad_step, 0)
        part = pl.ds(i * per_part, per_part)
        copies.append(pltpu.make_async_copy(grad.at[part], grad_hbm.at[part], sem.at[i]))
        copies[-1].start()
    lax.fori_loop(0, capacity // UNROLL, hidden_step, 0)
    for j in range(col_blocks):
        for i in range(group // shard):
            row0 = pl.multiple_of(place[i], 16)
            hid[pl.ds(row0, shard), j * side : (j + 1) * side] = acc[j, i * shard : (i + 1) * shard, :].astype(hid.dtype)
    copies.append(pltpu.make_async_copy(hid, hid_hbm, sem.at[OUT_PARTS]))
    copies[-1].start()
    for copy in copies:
        copy.wait()


def call_blocks(table, place, pieces, plan, weights, cots, slots, width, shard, scale):
    capacity, side, _ = weights.shape
    group, ff_dev = cots[0].shape
    total = group * len(cots)
    cost = pl.CostEstimate(
        flops=2 * side * side * (group * capacity + total * slots),
        bytes_accessed=2 * (weights.size + slots * side * side + total * (width + ff_dev) + group * ff_dev),
        transcendentals=0,
    )
    return pl.pallas_call(
        functools.partial(block_kernel, plan, len(pieces), len(cots), shard, scale),
        out_shape=(
            jax.ShapeDtypeStruct((group, ff_dev), jnp.bfloat16),
            jax.ShapeDtypeStruct((slots, side, side), jnp.bfloat16),
        ),
        in_specs=[pl.BlockSpec(memory_space=pltpu.SMEM)] * 2
        + [pl.BlockSpec(memory_space=pltpu.VMEM)] * (len(pieces) + len(cots) + 1),
        out_specs=(pl.BlockSpec(memory_space=pltpu.HBM),) * 2,
        scratch_shapes=[
            pltpu.VMEM((total, width), jnp.bfloat16),
            pltpu.VMEM((total, ff_dev), jnp.bfloat16),
            pltpu.VMEM((ff_dev // side, group, side), jnp.float32),
            pltpu.VMEM((group, ff_dev), jnp.bfloat16),
            pltpu.VMEM((slots, side, side), jnp.bfloat16),
            pltpu.SemaphoreType.DMA((OUT_PARTS + 1,)),
        ],
        compiler_params=pltpu.CompilerParams(vmem_limit_bytes=VMEM_LIMIT),
        cost_estimate=cost,
        name="blocks",
    )(table, place, *pieces, *cots, weights)


def two_group_plan(table, count, tokens, cotangent, weights, scale):
    tok_dev, width = tokens.shape
    quarter = width // 4
    group, ff_dev = cotangent.shape
    capacity, side, _ = weights.shape
    slots = capacity // 2
    row, col = lax.axis_index("row"), lax.axis_index("col")
    x, core = col // 2, col % 2
    swap_y = functools.partial(lax.ppermute, axis_name="dp", perm=[(0, 1), (1, 0)])

    def over_y(bundle):
        value, parts = bundle
        return swap_y(value), [(not own, shard, at) for own, shard, at in parts]

    def over_x(bundle):
        value, parts = bundle
        moved = lax.ppermute(value, "col", [(0, 2), (2, 0), (1, 3), (3, 1)])
        return moved, [(own, shard, at ^ 1) for own, shard, at in parts]

    def over_core(bundle):
        value, parts = bundle
        moved = lax.ppermute(value, "col", [(0, 1), (1, 0), (2, 3), (3, 2)])
        return moved, [(own, shard, at ^ 2) for own, shard, at in parts]

    def over_z(bundle, shard):
        value, parts = bundle
        by = (0, 1, 3, 2)[shard]
        moved = lax.ppermute(value, "row", [(i, (i + by) % 4) for i in range(4)])
        return moved, [(own, shard, at) for own, _, at in parts]

    def join(*bundles):
        return jnp.concatenate([v for v, _ in bundles], 0), [p for _, parts in bundles for p in parts]

    def cut(bundle, i, j):
        return bundle[0][i * tok_dev : j * tok_dev], bundle[1][i:j]

    def after(bundle, *earlier):
        return lax.optimization_barrier((bundle[0], [e[0] for e in earlier]))[0], bundle[1]

    place = [((row + 4 - by) % 4) * tok_dev for by in (0, 1, 3, 2)]
    place += [(xx * 2 + cc) * quarter for xx, cc in ((x, core), (1 - x, core), (x, 1 - core), (1 - x, 1 - core))]
    place = jnp.stack(place + [count, lax.axis_index("dp") * slots]).astype(jnp.int32)
    mine = lax.dynamic_slice_in_dim(tokens, col * quarter, quarter, 1)

    mine = (mine, [(True, 0, 0)])
    other0 = over_y(mine)
    own3 = over_z(mine, 3)
    both = join(mine, other0)
    both1 = over_z(both, 1)
    both2 = over_z(both, 2)
    other3 = over_y(own3)
    cot_other = swap_y(after((cotangent, None), other3)[0])
    own2, other2 = cut(both2, 0, 1), cut(both2, 1, 2)
    first = join(own3, other0)
    first_x = over_x(first)
    both1_x = over_x(both1)
    own2_x = over_x(own2)
    last = join(other3, other2)
    other2_x = over_x(after(other2, both1))
    other3_x = over_y(after(cut(first_x, 0, 1), both1, own2_x))
    near = join(first, both1)
    settled, (table, place) = lax.optimization_barrier((near[0], (table, place)))
    core_a = over_core((settled, near[1]))
    core_b = over_core(join(first_x, both1_x, own2, own2_x))
    core_c = over_core(last)
    core_d = over_core(join(other2_x, other3_x))
    got = [first, both1, own2, first_x, both1_x, own2_x, core_a, core_b, last, other2_x, other3_x, core_c, core_d]
    pieces, plan = [tokens], [(0, 0, tok_dev, 0, None)]
    for value, parts in got:
        for i, (own, shard, at) in enumerate(parts):
            plan.append((len(pieces), i * tok_dev, tok_dev, (0 if own else group) + shard * tok_dev, 4 + at))
        pieces.append(value)
    assert len(plan) == 29
    return call_blocks(
        table, place, pieces, plan, weights, [cotangent, cot_other], slots, width, tok_dev, scale
    )


def on_device(tokens, cotangent, weight_blocks, block_rows, block_cols, block_count):
    groups, steps = lax.axis_size("dp"), lax.axis_size("row")
    tok_dev, width = tokens.shape
    group, ff_dev = cotangent.shape
    weights = weight_blocks[0]
    capacity, side, _ = weights.shape
    scale = 1.0 / (group * groups) ** 0.5
    table, count = jnp.concatenate([block_rows, block_cols], 0), block_count[0]
    if (groups, steps, lax.axis_size("col")) == (2, 4, 4):
        hidden, grad = two_group_plan(table, count, tokens, cotangent, weights, scale)
        return hidden, grad[None]
    gathered = lax.all_gather(tokens, "row", axis=0, tiled=True)
    zero = jnp.zeros((), jnp.int32)
    place = jnp.stack([zero, count, zero])
    plan = [(0, 0, group, 0, None)]
    hidden, partial = call_blocks(table, place, [gathered], plan, weights, [cotangent], capacity, width, group, scale)
    return hidden, lax.psum_scatter(partial[None], "dp", scatter_dimension=1, tiled=True)


def solution(mesh):
    in_specs = (
        P(("dp", "row"), None),
        P("dp", ("row", "col")),
        P(("row", "col"), None, None, None),
        P(("row", "col"), None),
        P(("row", "col"), None),
        P(("row", "col")),
    )
    out_specs = (P("dp", ("row", "col")), P(("row", "col"), "dp", None, None))
    return jax.shard_map(
        on_device, mesh=mesh, in_specs=in_specs, out_specs=out_specs, check_vma=False
    )
```

```python
import functools

import jax
import jax.numpy as jnp
from jax import lax
from jax.experimental import pallas as pl
from jax.experimental.pallas import tpu as pltpu
from jax.sharding import PartitionSpec as P

UNROLL = 48
OUT_PARTS = 1
VMEM_LIMIT = 24 << 20


def block_kernel(plan, n_pieces, n_cots, shard, scale, table, place, *refs):
    pieces, cots = refs[:n_pieces], refs[n_pieces : n_pieces + n_cots]
    w, hid_hbm, grad_hbm, tok, cot, acc, hid, grad, sem = refs[n_pieces + n_cots :]
    capacity, side = w.shape[0], w.shape[1]
    col_blocks, group = acc.shape[0], acc.shape[1]
    slots = grad.shape[0]
    live, slot0 = place[place.shape[0] - 2], place[place.shape[0] - 1]
    acc[...] = jnp.zeros_like(acc)
    for operand, first, rows, row0, at in plan:
        src = pieces[operand]
        if at is None:
            tok[row0 : row0 + rows, :] = src[first : first + rows, :]
        else:
            lane = pl.multiple_of(place[at], 128)
            tok[row0 : row0 + rows, pl.ds(lane, src.shape[1])] = src[first : first + rows, :]
    for g, src in enumerate(cots):
        for i in range(group // shard):
            at = g * group + i * shard
            cot[at : at + shard, :] = src[pl.ds(pl.multiple_of(place[i], 16), shard), :]

    def grad_step(step, carry):
        base = step * UNROLL
        for u in range(UNROLL):
            k = slot0 + base + u
            lane = pl.multiple_of(table[0, k] * side, side)
            col = pl.multiple_of(table[1, k] * side, side)
            product = lax.dot_general(
                tok[:, pl.ds(lane, side)],
                cot[:, pl.ds(col, side)],
                (((0,), (0,)), ((), ())),
                preferred_element_type=jnp.float32,
            )
            grad[base + u] = jnp.where(k < live, product * scale, 0.0).astype(grad.dtype)
        return carry

    def hidden_step(step, carry):
        base = step * UNROLL
        products = []
        for u in range(UNROLL):
            k = base + u
            lane = pl.multiple_of(table[0, k] * side, side)
            product = jnp.dot(tok[0:group, pl.ds(lane, side)], w[k], preferred_element_type=jnp.float32)
            products.append(jnp.where(k < live, product, 0.0))
        for u in range(UNROLL):
            col = table[1, base + u]
            acc[col] = acc[col] + products[u]
        return carry

    per_part = slots // OUT_PARTS
    copies = []
    for i in range(OUT_PARTS):
        lax.fori_loop(i * per_part // UNROLL, (i + 1) * per_part // UNROLL, grad_step, 0)
        part = pl.ds(i * per_part, per_part)
        copies.append(pltpu.make_async_copy(grad.at[part], grad_hbm.at[part], sem.at[i]))
        copies[-1].start()
    lax.fori_loop(0, capacity // UNROLL, hidden_step, 0)
    for j in range(col_blocks):
        for i in range(group // shard):
            row0 = pl.multiple_of(place[i], 16)
            hid[pl.ds(row0, shard), j * side : (j + 1) * side] = acc[j, i * shard : (i + 1) * shard, :].astype(hid.dtype)
    copies.append(pltpu.make_async_copy(hid, hid_hbm, sem.at[OUT_PARTS]))
    copies[-1].start()
    for copy in copies:
        copy.wait()


def call_blocks(table, place, pieces, plan, weights, cots, slots, width, shard, scale):
    capacity, side, _ = weights.shape
    group, ff_dev = cots[0].shape
    total = group * len(cots)
    cost = pl.CostEstimate(
        flops=2 * side * side * (group * capacity + total * slots),
        bytes_accessed=2 * (weights.size + slots * side * side + total * (width + ff_dev) + group * ff_dev),
        transcendentals=0,
    )
    return pl.pallas_call(
        functools.partial(block_kernel, plan, len(pieces), len(cots), shard, scale),
        out_shape=(
            jax.ShapeDtypeStruct((group, ff_dev), jnp.bfloat16),
            jax.ShapeDtypeStruct((slots, side, side), jnp.bfloat16),
        ),
        in_specs=[pl.BlockSpec(memory_space=pltpu.SMEM)] * 2
        + [pl.BlockSpec(memory_space=pltpu.VMEM)] * (len(pieces) + len(cots) + 1),
        out_specs=(pl.BlockSpec(memory_space=pltpu.HBM),) * 2,
        scratch_shapes=[
            pltpu.VMEM((total, width), jnp.bfloat16),
            pltpu.VMEM((total, ff_dev), jnp.bfloat16),
            pltpu.VMEM((ff_dev // side, group, side), jnp.float32),
            pltpu.VMEM((group, ff_dev), jnp.bfloat16),
            pltpu.VMEM((slots, side, side), jnp.bfloat16),
            pltpu.SemaphoreType.DMA((OUT_PARTS + 1,)),
        ],
        compiler_params=pltpu.CompilerParams(vmem_limit_bytes=VMEM_LIMIT),
        cost_estimate=cost,
        name="blocks",
    )(table, place, *pieces, *cots, weights)


def two_group_plan(table, count, tokens, cotangent, weights, scale):
    tok_dev, width = tokens.shape
    quarter = width // 4
    group, ff_dev = cotangent.shape
    capacity, side, _ = weights.shape
    slots = capacity // 2
    row, col = lax.axis_index("row"), lax.axis_index("col")
    x, core = col // 2, col % 2
    swap_y = functools.partial(lax.ppermute, axis_name="dp", perm=[(0, 1), (1, 0)])

    def over_y(bundle):
        value, parts = bundle
        return swap_y(value), [(not own, shard, at) for own, shard, at in parts]

    def over_x(bundle):
        value, parts = bundle
        moved = lax.ppermute(value, "col", [(0, 2), (2, 0), (1, 3), (3, 1)])
        return moved, [(own, shard, at ^ 1) for own, shard, at in parts]

    def over_core(bundle):
        value, parts = bundle
        moved = lax.ppermute(value, "col", [(0, 1), (1, 0), (2, 3), (3, 2)])
        return moved, [(own, shard, at ^ 2) for own, shard, at in parts]

    def over_z(bundle, shard):
        value, parts = bundle
        by = (0, 1, 3, 2)[shard]
        moved = lax.ppermute(value, "row", [(i, (i + by) % 4) for i in range(4)])
        return moved, [(own, shard, at) for own, _, at in parts]

    def join(*bundles):
        return jnp.concatenate([v for v, _ in bundles], 0), [p for _, parts in bundles for p in parts]

    def cut(bundle, i, j):
        return bundle[0][i * tok_dev : j * tok_dev], bundle[1][i:j]

    def after(bundle, *earlier):
        return lax.optimization_barrier((bundle[0], [e[0] for e in earlier]))[0], bundle[1]

    place = [((row + 4 - by) % 4) * tok_dev for by in (0, 1, 3, 2)]
    place += [(xx * 2 + cc) * quarter for xx, cc in ((x, core), (1 - x, core), (x, 1 - core), (1 - x, 1 - core))]
    place = jnp.stack(place + [count, lax.axis_index("dp") * slots]).astype(jnp.int32)
    mine = lax.dynamic_slice_in_dim(tokens, col * quarter, quarter, 1)

    mine = (mine, [(True, 0, 0)])
    other0 = over_y(mine)
    own3 = over_z(mine, 3)
    both = join(mine, other0)
    both1 = over_z(both, 1)
    both2 = over_z(both, 2)
    other3 = over_y(own3)
    cot_other = swap_y(after((cotangent, None), other3)[0])
    own2, other2 = cut(both2, 0, 1), cut(both2, 1, 2)
    first = join(own3, other0)
    first_x = over_x(first)
    both1_x = over_x(both1)
    own2_x = over_x(own2)
    last = join(other3, other2)
    other2_x = over_x(after(other2, both1, first_x))
    other3_x = over_y(after(cut(first_x, 0, 1), own2_x))
    near = join(first, both1)
    settled, (table, place) = lax.optimization_barrier((near[0], (table, place)))
    core_a = over_core((settled, near[1]))
    core_b = over_core(join(first_x, both1_x, own2, own2_x))
    core_c = over_core(last)
    core_d = over_core(join(other2_x, other3_x))
    got = [first, both1, own2, first_x, both1_x, own2_x, core_a, core_b, last, other2_x, other3_x, core_c, core_d]
    pieces, plan = [tokens], [(0, 0, tok_dev, 0, None)]
    for value, parts in got:
        for i, (own, shard, at) in enumerate(parts):
            plan.append((len(pieces), i * tok_dev, tok_dev, (0 if own else group) + shard * tok_dev, 4 + at))
        pieces.append(value)
    assert len(plan) == 29
    return call_blocks(
        table, place, pieces, plan, weights, [cotangent, cot_other], slots, width, tok_dev, scale
    )


def on_device(tokens, cotangent, weight_blocks, block_rows, block_cols, block_count):
    groups, steps = lax.axis_size("dp"), lax.axis_size("row")
    tok_dev, width = tokens.shape
    group, ff_dev = cotangent.shape
    weights = weight_blocks[0]
    capacity, side, _ = weights.shape
    scale = 1.0 / (group * groups) ** 0.5
    table, count = jnp.concatenate([block_rows, block_cols], 0), block_count[0]
    if (groups, steps, lax.axis_size("col")) == (2, 4, 4):
        hidden, grad = two_group_plan(table, count, tokens, cotangent, weights, scale)
        return hidden, grad[None]
    gathered = lax.all_gather(tokens, "row", axis=0, tiled=True)
    zero = jnp.zeros((), jnp.int32)
    place = jnp.stack([zero, count, zero])
    plan = [(0, 0, group, 0, None)]
    hidden, partial = call_blocks(table, place, [gathered], plan, weights, [cotangent], capacity, width, group, scale)
    return hidden, lax.psum_scatter(partial[None], "dp", scatter_dimension=1, tiled=True)


def solution(mesh):
    in_specs = (
        P(("dp", "row"), None),
        P("dp", ("row", "col")),
        P(("row", "col"), None, None, None),
        P(("row", "col"), None),
        P(("row", "col"), None),
        P(("row", "col")),
    )
    out_specs = (P("dp", ("row", "col")), P(("row", "col"), "dp", None, None))
    return jax.shard_map(
        on_device, mesh=mesh, in_specs=in_specs, out_specs=out_specs, check_vma=False
    )
```
